32 devices in a mesh: groups: 2 (over x), src: 16 (over z, y, core).
Axes of the slice: x: 2, y: 2, z: 4, core: 2. Of those that a mesh axis runs over, the one named last changes fastest.
Arguments:
- eigenvectors: bfloat16 [32, 2, 3, 16, 8, 4, 128], P('groups', None, None, 'src'), parts along dimension 0, may hold values from -0.71875 to 0.71875
- gauge_links: bfloat16 [32, 2, 2, 3, 3, 16, 8, 4], P('groups', None, None, None, None, 'src'), parts along dimension 0, may hold values from -2.5 to 2.5
- hop_path: int32 [4], P('groups'), parts along dimension 0, may hold values from 0 to 3, as said below
- spin_perm: int32 [4, 4], P('groups'), parts along dimension 0, may hold values from 0 to 3, each once within a row
- spin_phase: int32 [4, 4], P('groups'), parts along dimension 0, may hold values from 0 to 3
- perambulators: bfloat16 [32, 2, 512, 512], P('groups', None, 'src'), parts along dimension 0, may hold values from -0.1875 to 0.1875
- owned_times: int32 [32, 2], P('groups'), parts along dimension 0, may hold values from -1 to 15, as said below
Outputs:
- insertions: bfloat16 [64, 2, 2, 512, 512], P(('groups', 'src')), parts along dimension 0
The draws below stay inside these ranges and needn't reach their ends.
There are 2 independent parts, one for each index of `groups`. The reference program is written for one: setup_inputs(seed, part) draws one part's arguments, and reference() takes and returns one part's arrays. A program takes and returns all parts, laid end to end along the dimension named above; each array names one. Nothing has to cross between parts.
Inputs may be any that keep to these rules, and one draw needn't show every extreme that they name: `hop_path`: codes 0, 1, 2, 3 stand for +y, -y, +z, -z; the 2 codes of the path are all different. `spin_perm`: each row is a permutation of the 4 spins. `owned_times`: every sink time 0 to 15 appears exactly once; a row lists its times first and then -1; a row lists at most 2 times, and some row exactly 2.
All inputs are finite; a program needn't handle non-finite values.
Results may differ from the reference program's by a relative error of at most 0.0058.
Values may be sent and summed in bfloat16 or wider, within the bound.
A program may use at most 128 MiB of HBM per device.

```python
import jax
import jax.numpy as jnp
from jax import lax

NVEC = 128
SPINS = 4
LY = 8
LZ = 4
NHOP = 2
NG = 2
TPD = 1
MOST = 2
LX = 16
NT = 16
N_SRC = 16


def draw_hop_path(key, part):
    base = jax.random.fold_in(key, 11)
    order = jax.random.permutation(base, 4).astype(jnp.int32)
    return order[:NHOP].astype(jnp.int32)


def draw_owned_times(key, part):
    base = jax.random.fold_in(key, 7)
    rank_key, time_key = jax.random.split(base)
    rank_order = jax.random.permutation(rank_key, N_SRC)
    heavy_count = N_SRC // 4
    counts = jnp.where(rank_order < heavy_count, MOST, jnp.where(rank_order < 2 * heavy_count, 0, TPD)).astype(jnp.int32)
    starts = jnp.cumsum(counts) - counts
    shuffled = jax.random.permutation(time_key, NT).astype(jnp.int32)
    slot_index = jnp.arange(MOST, dtype=jnp.int32)
    position = starts[:, None] + slot_index[None, :]
    picked = shuffled[jnp.clip(position, 0, NT - 1)]
    return jnp.where(slot_index[None, :] < counts[:, None], picked, -1).astype(jnp.int32)


def plant(drawn, key, low, top_value):
    spot = [jax.random.randint(jax.random.fold_in(key, axis), (), 0, length) for axis, length in enumerate(drawn.shape)]
    main_axis = drawn.shape.index(max(drawn.shape))
    neighbour = spot[:main_axis] + [(spot[main_axis] + 1) % drawn.shape[main_axis]] + spot[main_axis + 1:]
    return drawn.at[tuple(spot)].set(low).at[tuple(neighbour)].set(top_value)


def shard_levels(rng, dims, cuts, least, high):
    factor_of = 1.0
    for dim, shards_of in cuts:
        heights = jax.random.uniform(jax.random.fold_in(jax.random.fold_in(rng, 6), dim), (shards_of,), jnp.float32, least / len(cuts), high / len(cuts))
        factor_of = factor_of * jnp.repeat(jnp.exp(heights), dims[dim] // shards_of).reshape((-1,) + (1,) * (len(dims) - 1 - dim))
    return factor_of


def gaussian(rng, dims, deviation, bound, pieces=(), kind=jnp.bfloat16):
    factor_of = shard_levels(rng, dims, pieces, -0.22, 0.18) if pieces else 1.0
    result = jax.random.normal(rng, dims, jnp.float32) * deviation * factor_of
    return jnp.minimum(jnp.maximum(result, -bound), bound).astype(kind)


def setup_inputs(seed: int = 0, part: int = 0) -> dict:
    arg_keys = jax.random.split(jax.random.key(seed), 8)
    own_keys = jax.random.split(jax.random.fold_in(arg_keys[7], part), 8)
    return {
        "eigenvectors": gaussian(own_keys[0], (NT, 2, 3, LX, LY, LZ, NVEC), 0.12, 0.71875, ((3, 16),)),
        "gauge_links": gaussian(own_keys[1], (NT, 2, 2, 3, 3, LX, LY, LZ), 6 ** -0.5, 2.5, ((5, 16),)),
        "hop_path": draw_hop_path(jax.random.fold_in(jax.random.fold_in(arg_keys[7], part), 71), part),
        "spin_perm": jax.vmap(lambda own: jax.random.permutation(own, SPINS))(jax.random.split(own_keys[3], NG)).reshape((NG, SPINS)).astype(jnp.int32),
        "spin_phase": plant(jax.random.randint(own_keys[4], (NG, SPINS), 0, 4), jax.random.fold_in(own_keys[4], 1), 0, 3).astype(jnp.int32),
        "perambulators": gaussian(own_keys[5], (NT, 2, SPINS * NVEC, SPINS * NVEC), (2 * SPINS * NVEC) ** -0.5, 0.1875, ((2, 16),)),
        "owned_times": draw_owned_times(jax.random.fold_in(jax.random.fold_in(arg_keys[7], part), 71), part),
    }


def select_four(direction, first_case, second_case, third_case, fourth_case):
    return jnp.where(direction == 0, first_case, jnp.where(direction == 1, second_case, jnp.where(direction == 2, third_case, fourth_case)))


def adjoint(matrix):
    return jnp.stack([jnp.swapaxes(matrix[:, 0], 1, 2), -jnp.swapaxes(matrix[:, 1], 1, 2)], 1)


def displace(vectors, gauge_links, direction):
    forward_y = gauge_links[:, 0]
    forward_z = gauge_links[:, 1]
    link_pick = select_four(direction, forward_y, adjoint(jnp.roll(forward_y, 1, 5)), forward_z, adjoint(jnp.roll(forward_z, 1, 6)))
    displaced = select_four(direction, jnp.roll(vectors, -1, 4), jnp.roll(vectors, 1, 4), jnp.roll(vectors, -1, 5), jnp.roll(vectors, 1, 5))
    link_re = link_pick[:, 0].astype(jnp.float32)
    link_im = link_pick[:, 1].astype(jnp.float32)
    moved_re = displaced[:, 0].astype(jnp.float32)
    moved_im = displaced[:, 1].astype(jnp.float32)
    form = 'tcdxyz,tdxyzn->tcxyzn'
    real_part = jnp.einsum(form, link_re, moved_re) - jnp.einsum(form, link_im, moved_im)
    imag_part = jnp.einsum(form, link_re, moved_im) + jnp.einsum(form, link_im, moved_re)
    return lax.optimization_barrier(jnp.stack([real_part, imag_part], 1).astype(jnp.bfloat16))


def triple(stored, elemental, spin_perm, phase_re, phase_im):
    order = SPINS * NVEC
    stored_f = stored.astype(jnp.float32)
    columns = stored_f.reshape(2, order, SPINS, NVEC)
    permuted = jnp.take(columns, spin_perm, axis=2)
    products = jnp.einsum('kab,jdgsb->kjgdsa', elemental.astype(jnp.float32), permuted)
    real_part = products[0, 0] - products[1, 1]
    imag_part = products[0, 1] + products[1, 0]
    scale_re = phase_re[:, None, :, None]
    scale_im = phase_im[:, None, :, None]
    inserted = jnp.stack([scale_re * real_part - scale_im * imag_part, scale_re * imag_part + scale_im * real_part], 0)
    inserted = lax.optimization_barrier(inserted.reshape(2, NG, order, order).astype(jnp.bfloat16))
    outer = jnp.einsum('kcr,jgdr->kjgcd', stored_f, inserted.astype(jnp.float32))
    return jnp.stack([outer[0, 0] + outer[1, 1], outer[0, 1] - outer[1, 0]], 1).astype(jnp.bfloat16)


def reference(eigenvectors, gauge_links, hop_path, spin_perm, spin_phase, perambulators, owned_times):
    shifted = eigenvectors
    for hop_index in range(NHOP):
        shifted = displace(shifted, gauge_links, hop_path[hop_index])
    eigen_rows = eigenvectors.reshape(NT, 2, -1, NVEC).astype(jnp.float32)
    moved_rows = shifted.reshape(NT, 2, -1, NVEC).astype(jnp.float32)
    products = jnp.einsum('tkra,tjrb->tkjab', eigen_rows, moved_rows)
    elemental = jnp.stack([products[:, 0, 0] + products[:, 1, 1], products[:, 0, 1] - products[:, 1, 0]], 1)
    elemental = lax.optimization_barrier(elemental.astype(jnp.bfloat16))
    phase_re = (spin_phase == 0).astype(jnp.float32) - (spin_phase == 2).astype(jnp.float32)
    phase_im = (spin_phase == 1).astype(jnp.float32) - (spin_phase == 3).astype(jnp.float32)

    def one_time(time_pair):
        return triple(time_pair[0], time_pair[1], spin_perm, phase_re, phase_im)

    per_time = lax.map(one_time, (perambulators, elemental))
    slot_times = owned_times.reshape(-1)
    picked = jnp.take(per_time, jnp.clip(slot_times, 0, NT - 1).astype(jnp.int32), axis=0)
    filled = (slot_times >= 0)[:, None, None, None, None]
    return jnp.where(filled, picked, jnp.zeros_like(picked))
```

```python
import functools

import jax
import jax.numpy as jnp
import numpy as np
from jax import lax
from jax.experimental import pallas as pl
from jax.experimental.pallas import tpu as pltpu
from jax.sharding import PartitionSpec as P

F32 = jnp.float32
BF16 = jnp.bfloat16
QUAD = 4


def site_tables(side_y, side_z):
    sites = side_y * side_z
    site = np.arange(sites)
    ypos, zpos = site // side_z, site % side_z
    up_y = ((ypos + 1) % side_y) * side_z + zpos
    up_z = ypos * side_z + (zpos + 1) % side_z
    masks, movers = [], []
    for target in (up_y, up_z):
        up = (target[:, None] == site[None, :]).astype(np.float32)
        masks += [up, up.T]
        movers += [up, np.eye(sites, dtype=np.float32)]
    masks = np.stack([np.tile(m, (1, 3)) for m in masks])
    movers = np.stack([np.kron(np.eye(3, dtype=np.float32), m) for m in movers])
    return masks, movers


def flip(index, mask):
    result, bit = index, 1
    while bit <= mask:
        if mask & bit:
            result = result + bit - 2 * bit * lax.rem(index // bit, 2)
        bit *= 2
    return result


def exchange_kernel(
    n, hops, room, owned_ref, hop_ref, pera_hbm, eig_hbm, links_hbm, masks_hbm, movers_hbm,
    blocks_ref, elem_ref,
    pera_ref, eig_ref, links_ref, masks_ref, movers_ref, table, place, zstage, zland, fstage, mine, rows_ref, hopmask,
    esend, work, full, ypart, halves, across, pick, picked,
    fetch, give, take, zsend, zrecv, fsend, frecv, flocal, ysend, yrecv, hsend, hrecv, asend, arecv, gsend, grecv, psend, precv,
):
    slots = blocks_ref.shape[0]
    time_count = pera_ref.shape[0]
    rings = n // QUAD
    half, quarter = time_count // 2, time_count // 4
    me, group = lax.axis_index("src"), lax.axis_index("groups")
    mine_q, mine_z = lax.rem(me, QUAD), me // QUAD
    core, side = lax.rem(mine_q, 2), mine_q // 2
    sort = core * 2 + side
    levels = rings.bit_length() - 1

    def at_quad(mask):
        return (group, mine_z * QUAD + flip(mine_q, mask))

    def at_ring(mask):
        return (group, flip(mine_z, mask) * QUAD + mine_q)

    def remote(src, dst, send, recv, device):
        return pltpu.make_async_remote_copy(src_ref=src, dst_ref=dst, send_sem=send, recv_sem=recv, device_id=device)

    pairs = (
        (pera_hbm, pera_ref), (links_hbm, links_ref.at[0]), (masks_hbm, masks_ref), (movers_hbm, movers_ref),
        (eig_hbm.at[pl.ds(core * half, half)], eig_ref.at[0]),
    )
    fetches = [pltpu.make_async_copy(src, dst, fetch.at[i]) for i, (src, dst) in enumerate(pairs)]
    for copy in fetches:
        copy.start()

    barrier = pltpu.get_barrier_semaphore()
    for mask in range(1, QUAD):
        pl.semaphore_signal(barrier, inc=1, device_id=at_quad(mask))
    for mask in range(1, rings):
        pl.semaphore_signal(barrier, inc=1, device_id=at_ring(mask))

    @pl.loop(0, rings)
    def _(z):
        count = jnp.int32(0)
        found = [jnp.int32(0)] * room
        for s in range(slots):
            for q in range(QUAD):
                time = owned_ref[s, z * QUAD + q]
                filled = time >= 0
                place[s, z * QUAD + q] = jnp.minimum(count, room - 1)
                for j in range(min(room, s * QUAD + q + 1)):
                    found[j] = jnp.where(jnp.logical_and(filled, count == j), time, found[j])
                count = count + filled.astype(jnp.int32)
        for j in range(room):
            table[z, j] = found[j]

    fetches[0].wait()

    def stage_ring(mask):
        z = flip(mine_z, mask)
        for j in range(room):
            zstage[mask - 1, j] = pera_ref[table[z, j]]

    spans = ((0, QUAD), (QUAD, room - QUAD))

    def ring_copy(mask, part):
        first, size = spans[part]
        return remote(
            zstage.at[mask - 1, pl.ds(first, size)], zland[mask - 1][part],
            zsend.at[mask - 1, part], zrecv.at[mask - 1, part], at_ring(mask),
        )

    def quad_copy(ring, mask, s, receive):
        column = flip(mine_z, ring) * QUAD + (flip(mine_q, mask) if receive else mine_q)
        target = flip(mine_z, ring) * QUAD + mine_q
        return remote(
            fstage.at[ring, mask - 1, s], blocks_ref.at[s, column if receive else target],
            fsend.at[ring, mask - 1, s], frecv.at[ring, mask - 1, s], at_quad(mask),
        )

    def own_copy(ring, s):
        target = flip(mine_z, ring) * QUAD + mine_q
        return pltpu.make_async_copy(mine.at[ring, s], blocks_ref.at[s, target], flocal.at[ring, s])

    def forward(ring, s):
        def entry(q):
            at = place[s, mine_z * QUAD + q]
            if ring == 0:
                return pera_ref[table[mine_z, at]]
            first, rest = zland[ring - 1]
            value = first[jnp.minimum(at, QUAD - 1)]
            if s > 0:
                value = jnp.where(at < QUAD, value, rest[jnp.maximum(at - QUAD, 0)])
            return value

        for mask in range(1, QUAD):
            fstage[ring, mask - 1, s] = entry(flip(mine_q, mask))
            quad_copy(ring, mask, s, False).start()
        mine[ring, s] = entry(mine_q)
        own_copy(ring, s).start()

    pl.semaphore_wait(barrier, QUAD + rings - 2)
    shares = [
        remote(eig_hbm.at[pl.ds((1 - core) * half, half)], eig_ref.at[1], give.at[0], take.at[0], at_quad(1)),
        remote(links_hbm, links_ref.at[1], give.at[1], take.at[1], at_quad(1)),
    ]
    for copy in shares:
        copy.start()
    early = [m for m in range(1, rings) if m != rings // 2]
    for mask in reversed(early):
        stage_ring(mask)
        for part in range(2):
            ring_copy(mask, part).start()
    for s in range(slots):
        forward(0, s)
    stage_ring(rings // 2)

    for copy in fetches[1:]:
        copy.wait()
    for copy in shares:
        copy.wait()
    for h in range(hops):
        code = hop_ref[h]
        chosen = [(code == i).astype(F32) for i in range(4)]
        hopmask[h] = sum(chosen[i] * masks_ref[i] for i in range(4))
        mover = sum(chosen[i] * movers_ref[i] for i in range(4)).astype(BF16)
        for plane in range(2):
            for k in range(2):
                sign = 1.0 - 2.0 * k
                for c in range(3):
                    stack = []
                    for d in range(3):
                        here, there = k * 9 + c * 3 + d, k * 9 + d * 3 + c
                        stack.append(
                            chosen[0] * links_ref[plane, here].astype(F32)
                            + (sign * chosen[1]) * links_ref[plane, there].astype(F32)
                            + chosen[2] * links_ref[plane, 18 + here].astype(F32)
                            + (sign * chosen[3]) * links_ref[plane, 18 + there].astype(F32)
                        )
                    rows_ref[plane, h, k * 3 + c] = lax.dot_general(
                        jnp.concatenate(stack, 0).astype(BF16), mover, (((0,), (0,)), ((), ())),
                        preferred_element_type=F32,
                    )

    def one_plane(plane, i):
        vec = eig_ref[plane, i]
        cur = vec
        mid = vec.shape[0] // 2
        for h in range(hops):
            mask = hopmask[h]
            row = [rows_ref[plane, h, j, pl.ds(core * half + i, 1), :] for j in range(6)]
            re = jnp.concatenate([mask * row[c] for c in range(3)], 0)
            im = jnp.concatenate([mask * row[3 + c] for c in range(3)], 0)
            re, im, neg = re.astype(BF16), im.astype(BF16), (-im).astype(BF16)
            top, low = cur[:mid], cur[mid:]
            out_re = jnp.dot(re, top, preferred_element_type=F32) + jnp.dot(neg, low, preferred_element_type=F32)
            out_im = jnp.dot(im, top, preferred_element_type=F32) + jnp.dot(re, low, preferred_element_type=F32)
            cur = jnp.concatenate([out_re, out_im], 0).astype(BF16)
        turned = jnp.concatenate([cur[mid:], -cur[:mid]], 0)
        return vec, jnp.concatenate([cur, turned], 1)

    def one_time(i):
        left, right = zip(*(one_plane(plane, i) for plane in range(2)))
        return lax.dot_general(
            jnp.concatenate(left, 0), jnp.concatenate(right, 0), (((0,), (0,)), ((), ())), preferred_element_type=F32
        ).astype(BF16)

    def theirs(k, carry):
        esend[k] = one_time((1 - side) * quarter + k)
        return carry

    def ours(k, carry):
        work[k] = one_time(side * quarter + k)
        return carry

    lax.fori_loop(0, quarter, theirs, 0, unroll=4)
    y_copy = remote(esend, ypart, ysend.at[0], yrecv.at[0], at_quad(2))
    y_copy.start()
    lax.fori_loop(0, quarter, ours, 0, unroll=4)

    def add(target, base, extra, count):
        for i in range(count):
            target[base + i] = (work[base + i].astype(F32) + extra[i].astype(F32)).astype(BF16)

    y_copy.wait()
    add(work, 0, ypart, quarter)
    low, size = 0, quarter
    held = []
    waiting = list(reversed(early))
    for level in range(levels - 1):
        size //= 2
        bit = lax.rem(mine_z // 2**level, 2)
        keep, away = low + bit * size, low + (1 - bit) * size
        copy = remote(
            work.at[pl.ds(away, size)], halves.at[level, pl.ds(0, size)], hsend.at[level], hrecv.at[level], at_ring(2**level)
        )
        copy.start()
        if level == 0:
            for part in range(2):
                ring_copy(1, part).wait()
            for s in range(slots):
                forward(1, s)
            waiting.remove(1)
        copy.wait()
        add(work, keep, halves.at[level], size)
        held.append((keep, size))
        low = keep
    copy = remote(work.at[pl.ds(low, size)], across, asend.at[0], arecv.at[0], at_ring(rings // 2))
    copy.start()
    for part in range(2):
        ring_copy(rings // 2, part).start()
    copy.wait()
    add(full, low, across, size)
    for level in reversed(range(levels - 1)):
        keep, size = held[level]
        bit = lax.rem(mine_z // 2**level, 2)
        other = keep + (1 - 2 * bit) * size
        give_back = remote(
            full.at[pl.ds(keep, size)], full.at[pl.ds(keep, size)], gsend.at[level], grecv.at[level], at_ring(2**level)
        )
        give_back.start()
        if level == 0:
            for mask in waiting:
                for part in range(2):
                    ring_copy(mask, part).wait()
                for s in range(slots):
                    forward(mask, s)
        give_back.wait_send()
        remote(
            full.at[pl.ds(other, size)], full.at[pl.ds(other, size)], gsend.at[level], grecv.at[level], at_ring(2**level)
        ).wait_recv()

    def chosen_block(q, s):
        at = jnp.maximum(owned_ref[s, mine_z * QUAD + q], 0) - sort * quarter
        return full[jnp.minimum(jnp.maximum(at, 0), quarter - 1)]

    def pick_copy(mask, origin):
        return remote(pick.at[mask - 1], picked.at[origin], psend.at[mask - 1], precv.at[mask - 1], at_quad(mask))

    for mask in range(1, QUAD):
        for s in range(slots):
            pick[mask - 1, s] = chosen_block(flip(mine_q, mask), s)
        pick_copy(mask, mine_q).start()
    for s in range(slots):
        picked[mine_q, s] = chosen_block(mine_q, s)

    for s in range(slots):
        ring_copy(rings // 2, s).wait()
        forward(rings // 2, s)
    for mask in range(1, QUAD):
        pick_copy(mask, mine_q).wait_send()
        pick_copy(mask, flip(mine_q, mask)).wait_recv()
    for s in range(slots):
        kind = jnp.maximum(owned_ref[s, me], 0) // quarter
        elem_ref[s] = picked[lax.rem(kind, 2) * 2 + kind // 2, s]
    for ring in range(rings):
        for s in range(slots):
            for mask in range(1, QUAD):
                quad_copy(ring, mask, s, False).wait_send()
                quad_copy(ring, mask, s, True).wait_recv()
            own_copy(ring, s).wait()


def triple_kernel(perm_ref, phase_ref, owned_ref, blocks_ref, elem_ref, out_ref, left, turned):
    slot, group = pl.program_id(0), pl.program_id(1)
    order = out_ref.shape[-1]
    width = elem_ref.shape[1]
    spins = order // width

    @pl.when(group == 0)
    def _():
        elem = elem_ref[0]
        re = blocks_ref[0, :, 0].reshape(order, order)
        im = blocks_ref[0, :, 1].reshape(order, order)
        left[:, :order] = re
        left[:, order:] = im
        for spin in range(spins):
            part_re = re[:, spin * width : (spin + 1) * width]
            part_im = im[:, spin * width : (spin + 1) * width]
            dims = (((1,), (1,)), ((), ()))
            turned[spin, 0] = lax.dot_general(
                elem, jnp.concatenate([part_re, -part_im], 1), dims, preferred_element_type=F32
            ).astype(BF16)
            turned[spin, 1] = lax.dot_general(
                elem, jnp.concatenate([part_im, part_re], 1), dims, preferred_element_type=F32
            ).astype(BF16)

    reals, imags = [], []
    for spin in range(spins):
        source = perm_ref[group, spin]
        phase = phase_ref[group, spin]
        scale_re = (phase == 0).astype(F32) - (phase == 2).astype(F32)
        scale_im = (phase == 1).astype(F32) - (phase == 3).astype(F32)
        re = turned[source, 0].astype(F32)
        im = turned[source, 1].astype(F32)
        reals.append((scale_re * re - scale_im * im).astype(BF16))
        imags.append((scale_re * im + scale_im * re).astype(BF16))
    real, imag = jnp.concatenate(reals, 0), jnp.concatenate(imags, 0)
    filled = owned_ref[slot, lax.axis_index("src")] >= 0
    lhs = left[...]
    for part, right in enumerate((jnp.concatenate([real, imag], 0), jnp.concatenate([imag, -real], 0))):
        result = jnp.dot(lhs, right, preferred_element_type=F32)
        out_ref[0, 0, part] = jnp.where(filled, result, 0.0).astype(BF16)


def shards(n, eigenvectors, gauge_links, hop_path, spin_perm, spin_phase, perambulators, owned_times):
    time_count = eigenvectors.shape[0]
    width = eigenvectors.shape[-1]
    slots = owned_times.shape[1]
    rows, order = perambulators.shape[2], perambulators.shape[3]
    groups = spin_perm.shape[0]
    hops = hop_path.shape[0]
    rings = n // QUAD
    side_y, side_z = eigenvectors.shape[4], eigenvectors.shape[5]
    sites = side_y * side_z
    eig = eigenvectors.reshape(time_count, -1, width)
    links = jnp.transpose(gauge_links.reshape(time_count, 36, sites), (1, 2, 0))
    masks, movers = site_tables(side_y, side_z)
    tile = (width, 2 * width)
    half, quarter = time_count // 2, time_count // 4
    levels = rings.bit_length() - 1
    block = (2, rows, order)
    vmem = pl.BlockSpec(memory_space=pltpu.VMEM)
    smem = pl.BlockSpec(memory_space=pltpu.SMEM)
    arrays = (perambulators, eig, links, jnp.asarray(masks), jnp.asarray(movers))

    def exchange(room):
        def scratch(*shape):
            return pltpu.VMEM(shape, BF16)

        def both(*shape):
            return [pltpu.SemaphoreType.DMA(shape)] * 2

        return pl.pallas_call(
            functools.partial(exchange_kernel, n, hops, room),
            out_shape=(
                jax.ShapeDtypeStruct((slots, n) + block, BF16),
                jax.ShapeDtypeStruct((slots,) + tile, BF16),
            ),
            in_specs=[smem, smem] + [pl.BlockSpec(memory_space=pltpu.HBM)] * 5,
            out_specs=(pl.BlockSpec(memory_space=pl.ANY), vmem),
            scratch_shapes=[
                scratch(*perambulators.shape),
                scratch(2, half, *eig.shape[1:]),
                scratch(2, *links.shape),
                pltpu.VMEM(masks.shape, F32),
                pltpu.VMEM(movers.shape, F32),
                pltpu.SMEM((rings, room), jnp.int32),
                pltpu.SMEM((slots, n), jnp.int32),
                scratch(rings - 1, room, *block),
                [[scratch(QUAD, *block), scratch(room - QUAD, *block)] for _ in range(rings - 1)],
                scratch(rings, QUAD - 1, slots, *block),
                scratch(rings, slots, *block),
                pltpu.VMEM((2, hops, 6, time_count, 3 * sites), F32),
                pltpu.VMEM((hops, sites, 3 * sites), F32),
                scratch(quarter, *tile),
                scratch(quarter, *tile),
                scratch(quarter, *tile),
                scratch(quarter, *tile),
                scratch(max(levels - 1, 1), quarter // 2, *tile),
                scratch(2 * quarter // rings, *tile),
                scratch(QUAD - 1, slots, *tile),
                scratch(QUAD, slots, *tile),
                pltpu.SemaphoreType.DMA((5,)),
            ]
            + both(2)
            + both(rings - 1, 2)
            + both(rings, QUAD - 1, slots)
            + [pltpu.SemaphoreType.DMA((rings, slots))]
            + both(1)
            + both(levels)
            + both(1)
            + both(levels)
            + both(QUAD - 1),
            compiler_params=pltpu.CompilerParams(
                collective_id=room, has_side_effects=True, vmem_limit_bytes=56 * 2**20
            ),
            name=f"exchange{room}",
        )

    least, most = QUAD + 1, QUAD * slots
    filled = (owned_times.reshape(rings, -1) >= 0).astype(jnp.int32)
    worst = jnp.max(jnp.sum(filled, 1))
    blocks, elem = lax.switch(
        jnp.clip(worst - least, 0, most - least),
        [exchange(room) for room in range(least, most + 1)],
        owned_times.T, hop_path, *arrays,
    )
    return pl.pallas_call(
        triple_kernel,
        grid=(slots, groups),
        out_shape=jax.ShapeDtypeStruct((slots, groups, 2, order, order), BF16),
        in_specs=[
            smem,
            smem,
            smem,
            pl.BlockSpec((1, n, 2, rows, order), lambda s, g: (s, 0, 0, 0, 0)),
            pl.BlockSpec((1, width, 2 * width), lambda s, g: (s, 0, 0)),
        ],
        out_specs=pl.BlockSpec((1, 1, 2, order, order), lambda s, g: (s, g, 0, 0, 0)),
        scratch_shapes=[
            pltpu.VMEM((order, 2 * order), BF16),
            pltpu.VMEM((order // width, 2, width, order), BF16),
        ],
        compiler_params=pltpu.CompilerParams(
            dimension_semantics=("arbitrary", "arbitrary"), vmem_limit_bytes=56 * 2**20
        ),
        name="triple",
    )(spin_perm, spin_phase, owned_times.T, blocks, elem)


def solution(mesh):
    in_specs = (
        P("groups", None, None, "src", None, None, None),
        P("groups", None, None, None, None, "src", None, None),
        P("groups"),
        P("groups", None),
        P("groups", None),
        P("groups", None, "src", None),
        P("groups", None),
    )
    out_specs = P(("groups", "src"), None, None, None, None)
    return jax.shard_map(
        functools.partial(shards, mesh.shape["src"]),
        mesh=mesh, in_specs=in_specs, out_specs=out_specs, check_vma=False,
    )
```

```python
import functools

import jax
import jax.numpy as jnp
import numpy as np
from jax import lax
from jax.experimental import pallas as pl
from jax.experimental.pallas import tpu as pltpu
from jax.sharding import PartitionSpec as P

F32 = jnp.float32
BF16 = jnp.bfloat16
QUAD = 4


def site_tables(side_y, side_z):
    sites = side_y * side_z
    site = np.arange(sites)
    ypos, zpos = site // side_z, site % side_z
    up_y = ((ypos + 1) % side_y) * side_z + zpos
    up_z = ypos * side_z + (zpos + 1) % side_z
    masks, movers = [], []
    for target in (up_y, up_z):
        up = (target[:, None] == site[None, :]).astype(np.float32)
        masks += [up, up.T]
        movers += [up, np.eye(sites, dtype=np.float32)]
    masks = np.stack([np.tile(m, (1, 6)) for m in masks])
    movers = np.stack([np.kron(np.eye(6, dtype=np.float32), m) for m in movers])
    return masks, movers


def flip(index, mask):
    result, bit = index, 1
    while bit <= mask:
        if mask & bit:
            result = result + bit - 2 * bit * lax.rem(index // bit, 2)
        bit *= 2
    return result


def schedule(rings):
    far = rings // 2
    rest = [m for m in reversed(range(2, rings)) if m != far]

    def each(step, masks):
        return [(step, m, part) for m in masks for part in range(2)]

    return (
        (each("send", rest + [far]), each("send", rest + [1])),
        each("pass", [0]) + [("theirs",), ("ours",), ("join",)],
        (each("send", [1]) + each("pass", rest), each("pass", [far])),
        [("cross",)],
        (each("pass", [1]), each("send", [far]) + each("pass", [1] + rest)),
        [("spread",)],
        (each("pass", [far]), []),
        [("collect",)],
    )


def exchange_kernel(
    n, hops, room, owned_ref, hop_ref, pera_hbm, eig_hbm, links_hbm, masks_hbm, movers_hbm,
    blocks_ref, elem_ref,
    pera_ref, eig_ref, links_ref, masks_ref, movers_ref, table, place, zstage, zland, fstage, mine, rows_ref, hopmask,
    esend, work, ypart, joined, across, whole, picked,
    fetch, give, take, zsend, zrecv, fsend, frecv, flocal, ysend, yrecv, jsend, jrecv, csend, crecv, psend, precv,
):
    slots = blocks_ref.shape[0]
    time_count = pera_ref.shape[0]
    rings = n // QUAD
    share = rings * room // QUAD
    most = -(-room // QUAD)
    me, group = lax.axis_index("src"), lax.axis_index("groups")
    mine_q, mine_z = lax.rem(me, QUAD), me // QUAD

    def at_quad(mask):
        return (group, mine_z * QUAD + flip(mine_q, mask))

    def at_ring(mask):
        return (group, flip(mine_z, mask) * QUAD + mine_q)

    def remote(src, dst, send, recv, device):
        return pltpu.make_async_remote_copy(src_ref=src, dst_ref=dst, send_sem=send, recv_sem=recv, device_id=device)

    pairs = (
        (pera_hbm, pera_ref), (links_hbm, links_ref.at[0]), (masks_hbm, masks_ref), (movers_hbm, movers_ref),
        (eig_hbm, eig_ref.at[0]),
    )
    fetches = [pltpu.make_async_copy(src, dst, fetch.at[i]) for i, (src, dst) in enumerate(pairs)]
    for copy in fetches:
        copy.start()

    barrier = pltpu.get_barrier_semaphore()
    for mask in range(1, QUAD):
        pl.semaphore_signal(barrier, inc=1, device_id=at_quad(mask))
    for mask in range(1, rings):
        pl.semaphore_signal(barrier, inc=1, device_id=at_ring(mask))

    @pl.loop(0, rings)
    def _(z):
        count = jnp.int32(0)
        found = [jnp.int32(0)] * room
        for s in range(slots):
            for q in range(QUAD):
                time = owned_ref[s, z * QUAD + q]
                filled = time >= 0
                place[s, z * QUAD + q] = jnp.minimum(count, room - 1)
                for j in range(min(room, s * QUAD + q + 1)):
                    found[j] = jnp.where(jnp.logical_and(filled, count == j), time, found[j])
                count = count + filled.astype(jnp.int32)
        for j in range(room):
            table[z * room + j] = found[j]

    fetches[0].wait()

    def stage_ring(mask):
        z = flip(mine_z, mask)
        for j in range(room):
            zstage[mask - 1, j] = pera_ref[table[z * room + j]]

    spans = ((0, QUAD), (QUAD, room - QUAD))

    def ring_copy(mask, part):
        first, size = spans[part]
        return remote(
            zstage.at[mask - 1, pl.ds(first, size)], zland[mask - 1][part],
            zsend.at[mask - 1, part], zrecv.at[mask - 1, part], at_ring(mask),
        )

    def quad_copy(ring, mask, s, receive):
        column = flip(mine_z, ring) * QUAD + (flip(mine_q, mask) if receive else mine_q)
        target = flip(mine_z, ring) * QUAD + mine_q
        return remote(
            fstage.at[ring, mask - 1, s], blocks_ref.at[s, column if receive else target],
            fsend.at[ring, mask - 1, s], frecv.at[ring, mask - 1, s], at_quad(mask),
        )

    def own_copy(ring, s):
        target = flip(mine_z, ring) * QUAD + mine_q
        return pltpu.make_async_copy(mine.at[ring, s], blocks_ref.at[s, target], flocal.at[ring, s])

    def forward(ring, s):
        def entry(q):
            at = place[s, mine_z * QUAD + q]
            if ring == 0:
                return pera_ref[table[mine_z * room + at]]
            first, rest = zland[ring - 1]
            value = first[jnp.minimum(at, QUAD - 1)]
            if s > 0:
                value = jnp.where(at < QUAD, value, rest[jnp.maximum(at - QUAD, 0)])
            return value

        for mask in range(1, QUAD):
            fstage[ring, mask - 1, s] = entry(flip(mine_q, mask))
            quad_copy(ring, mask, s, False).start()
        mine[ring, s] = entry(mine_q)
        own_copy(ring, s).start()

    pl.semaphore_wait(barrier, QUAD + rings - 2)
    shares = [
        remote(eig_hbm, eig_ref.at[1], give.at[0], take.at[0], at_quad(1)),
        remote(links_hbm, links_ref.at[1], give.at[1], take.at[1], at_quad(1)),
    ]
    for copy in shares:
        copy.start()
    def send_ring(mask, part):
        if part == 0:
            stage_ring(mask)
        ring_copy(mask, part).start()

    def pass_on(mask, s):
        if mask:
            ring_copy(mask, s).wait_recv()
        forward(mask, s)

    def one_plane(plane, time):
        vec = eig_ref[plane, time]
        cur = vec
        mid = vec.shape[0] // 2
        for h in range(hops):
            mask = hopmask[h]
            hop = [mask * rows_ref[plane, h, j, pl.ds(time, 1), :] for j in range(6)]
            cur = jnp.dot(jnp.concatenate(hop, 0).astype(BF16), cur, preferred_element_type=F32).astype(BF16)
        turned = jnp.concatenate([cur[mid:], -cur[:mid]], 0)
        return vec, jnp.concatenate([cur, turned], 1)

    def one_entry(entry):
        time = table[entry]
        left, right = zip(*(one_plane(plane, time) for plane in range(2)))
        return lax.dot_general(
            jnp.concatenate(left, 0), jnp.concatenate(right, 0), (((0,), (0,)), ((), ())), preferred_element_type=F32
        ).astype(BF16)

    def theirs(i, carry):
        esend[i] = one_entry(QUAD * i + flip(mine_q, 2))
        return carry

    def ours(i, carry):
        work[i] = one_entry(QUAD * i + mine_q)
        return carry

    y_copy = remote(esend, ypart, ysend.at[0], yrecv.at[0], at_quad(2))

    def row_of(i):
        return (QUAD * i + mine_q) // room

    def first_of(z):
        return (z * room - mine_q + QUAD - 1) // QUAD

    def even(i):
        return lax.rem(row_of(i) + mine_z, 2) == 0

    def join_copy(i):
        return remote(work.at[i], joined.at[i], jsend.at[i], jrecv.at[i], at_ring(1))

    def cross_copy(i):
        z = row_of(i)
        at = i - first_of(z)
        return remote(work.at[i], across.at[mine_z, at], csend.at[i], crecv.at[mine_z, at], (group, z * QUAD + mine_q))

    def cross_land(z, at):
        return remote(work.at[0], across.at[z, at], csend.at[0], crecv.at[z, at], (group, z * QUAD + mine_q))

    def held(at):
        return first_of(mine_z) + at < first_of(mine_z + 1)

    def pick_copy(mask, origin, at):
        return remote(
            whole.at[at], picked.at[origin, at], psend.at[mask - 1, at], precv.at[mask - 1, at], at_quad(mask)
        )

    def compute_theirs():
        for copy in fetches[1:]:
            copy.wait()
        for copy in shares:
            copy.wait()
        for h in range(hops):
            code = hop_ref[h]
            chosen = [(code == i).astype(F32) for i in range(4)]
            hopmask[h] = sum(chosen[i] * masks_ref[i] for i in range(4))
            mover = sum(chosen[i] * movers_ref[i] for i in range(4)).astype(BF16)
            for plane in range(2):
                for k in range(2):
                    for c in range(3):
                        stack = []
                        for part in range(2):
                            kind = (k + part) % 2
                            turn = -1.0 if part == 1 and kind == 1 else 1.0
                            sign = turn * (1.0 - 2.0 * kind)
                            for d in range(3):
                                here, there = kind * 9 + c * 3 + d, kind * 9 + d * 3 + c
                                stack.append(
                                    (turn * chosen[0]) * links_ref[plane, here].astype(F32)
                                    + (sign * chosen[1]) * links_ref[plane, there].astype(F32)
                                    + (turn * chosen[2]) * links_ref[plane, 18 + here].astype(F32)
                                    + (sign * chosen[3]) * links_ref[plane, 18 + there].astype(F32)
                                )
                        rows_ref[plane, h, k * 3 + c] = lax.dot_general(
                            jnp.concatenate(stack, 0).astype(BF16), mover, (((0,), (0,)), ((), ())),
                            preferred_element_type=F32,
                        )

        lax.fori_loop(0, share, theirs, 0, unroll=2)
        y_copy.start()

    def compute_ours():
        lax.fori_loop(0, share, ours, 0, unroll=2)

    def join():
        y_copy.wait()

        @pl.loop(0, share)
        def _(i):
            @pl.when(jnp.logical_not(even(i)))
            def _():
                work[i] = (work[i].astype(F32) + ypart[i].astype(F32)).astype(BF16)
                join_copy(i).start()

    def cross():
        @pl.loop(0, share)
        def _(i):
            @pl.when(even(i))
            def _():
                join_copy(i).wait_recv()
                total = work[i].astype(F32) + ypart[i].astype(F32) + joined[i].astype(F32)
                work[i] = total.astype(BF16)

                @pl.when(row_of(i) != mine_z)
                def _():
                    cross_copy(i).start()

    def spread():
        for at in range(most):

            @pl.when(held(at))
            def _():
                total = work[first_of(mine_z) + at].astype(F32)
                for mask in range(2, rings, 2):
                    z = flip(mine_z, mask)
                    cross_land(z, at).wait_recv()
                    total += across[z, at].astype(F32)
                whole[at] = total.astype(BF16)
                for mask in range(1, QUAD):
                    pick_copy(mask, mine_q, at).start()
                picked[mine_q, at] = whole[at]

    def collect():
        @pl.loop(0, share)
        def _(i):
            @pl.when(jnp.logical_not(even(i)))
            def _():
                join_copy(i).wait_send()

            @pl.when(jnp.logical_and(even(i), row_of(i) != mine_z))
            def _():
                cross_copy(i).wait_send()

        for mask in range(1, QUAD):
            q = flip(mine_q, mask)
            for at in range(most):

                @pl.when(held(at))
                def _():
                    pick_copy(mask, mine_q, at).wait_send()

                @pl.when((mine_z * room - q + QUAD - 1) // QUAD + at < ((mine_z + 1) * room - q + QUAD - 1) // QUAD)
                def _():
                    pick_copy(mask, q, at).wait_recv()

        for s in range(slots):
            entry = mine_z * room + place[s, me]
            q = lax.rem(entry, QUAD)
            first = lax.div(mine_z * room - q + QUAD - 1, QUAD)
            elem_ref[s] = picked[q, jnp.maximum(lax.div(entry, QUAD) - first, 0)]

    actions = {
        "send": send_ring, "pass": pass_on, "theirs": compute_theirs, "ours": compute_ours, "join": join,
        "cross": cross, "spread": spread, "collect": collect,
    }

    def run(steps):
        for name, *rest in steps:
            actions[name](*rest)

    inner = jnp.logical_and(mine_z > 0, mine_z < rings - 1)
    for phase in schedule(rings):
        if isinstance(phase, tuple):
            pl.when(jnp.logical_not(inner))(functools.partial(run, phase[0]))
            pl.when(inner)(functools.partial(run, phase[1]))
        else:
            run(phase)

    for mask in range(1, rings):
        for part in range(2):
            ring_copy(mask, part).wait_send()
    for ring in range(rings):
        for s in range(slots):
            for mask in range(1, QUAD):
                quad_copy(ring, mask, s, False).wait_send()
                quad_copy(ring, mask, s, True).wait_recv()
            own_copy(ring, s).wait()


def triple_kernel(perm_ref, phase_ref, owned_ref, blocks_ref, elem_ref, out_ref, left, turned):
    slot, group = pl.program_id(0), pl.program_id(1)
    order = out_ref.shape[-1]
    width = elem_ref.shape[1]
    spins = order // width

    @pl.when(group == 0)
    def _():
        elem = elem_ref[0]
        re = blocks_ref[0, :, 0].reshape(order, order)
        im = blocks_ref[0, :, 1].reshape(order, order)
        left[:, :order] = re
        left[:, order:] = im
        for spin in range(spins):
            part_re = re[:, spin * width : (spin + 1) * width]
            part_im = im[:, spin * width : (spin + 1) * width]
            dims = (((1,), (1,)), ((), ()))
            turned[spin, 0] = lax.dot_general(
                elem, jnp.concatenate([part_re, -part_im], 1), dims, preferred_element_type=F32
            ).astype(BF16)
            turned[spin, 1] = lax.dot_general(
                elem, jnp.concatenate([part_im, part_re], 1), dims, preferred_element_type=F32
            ).astype(BF16)

    reals, imags = [], []
    for spin in range(spins):
        source = perm_ref[group, spin]
        phase = phase_ref[group, spin]
        scale_re = (phase == 0).astype(F32) - (phase == 2).astype(F32)
        scale_im = (phase == 1).astype(F32) - (phase == 3).astype(F32)
        re = turned[source, 0].astype(F32)
        im = turned[source, 1].astype(F32)
        reals.append((scale_re * re - scale_im * im).astype(BF16))
        imags.append((scale_re * im + scale_im * re).astype(BF16))
    real, imag = jnp.concatenate(reals, 0), jnp.concatenate(imags, 0)
    filled = owned_ref[slot, lax.axis_index("src")] >= 0
    lhs = left[...]
    for part, right in enumerate((jnp.concatenate([real, imag], 0), jnp.concatenate([imag, -real], 0))):
        result = jnp.dot(lhs, right, preferred_element_type=F32)
        out_ref[0, 0, part] = jnp.where(filled, result, 0.0).astype(BF16)


def shards(n, eigenvectors, gauge_links, hop_path, spin_perm, spin_phase, perambulators, owned_times):
    time_count = eigenvectors.shape[0]
    width = eigenvectors.shape[-1]
    slots = owned_times.shape[1]
    rows, order = perambulators.shape[2], perambulators.shape[3]
    groups = spin_perm.shape[0]
    hops = hop_path.shape[0]
    rings = n // QUAD
    side_y, side_z = eigenvectors.shape[4], eigenvectors.shape[5]
    sites = side_y * side_z
    eig = eigenvectors.reshape(time_count, -1, width)
    links = jnp.transpose(gauge_links.reshape(time_count, 36, sites), (1, 2, 0))
    masks, movers = site_tables(side_y, side_z)
    tile = (width, 2 * width)
    block = (2, rows, order)
    vmem = pl.BlockSpec(memory_space=pltpu.VMEM)
    smem = pl.BlockSpec(memory_space=pltpu.SMEM)
    arrays = (perambulators, eig, links, jnp.asarray(masks), jnp.asarray(movers))

    def exchange(room):
        share = rings * room // QUAD
        most = -(-room // QUAD)

        def scratch(*shape):
            return pltpu.VMEM(shape, BF16)

        def both(*shape):
            return [pltpu.SemaphoreType.DMA(shape)] * 2

        return pl.pallas_call(
            functools.partial(exchange_kernel, n, hops, room),
            out_shape=(
                jax.ShapeDtypeStruct((slots, n) + block, BF16),
                jax.ShapeDtypeStruct((slots,) + tile, BF16),
            ),
            in_specs=[smem, smem] + [pl.BlockSpec(memory_space=pltpu.HBM)] * 5,
            out_specs=(pl.BlockSpec(memory_space=pl.ANY), vmem),
            scratch_shapes=[
                scratch(*perambulators.shape),
                scratch(2, *eig.shape),
                scratch(2, *links.shape),
                pltpu.VMEM(masks.shape, F32),
                pltpu.VMEM(movers.shape, F32),
                pltpu.SMEM((rings * room,), jnp.int32),
                pltpu.SMEM((slots, n), jnp.int32),
                scratch(rings - 1, room, *block),
                [[scratch(QUAD, *block), scratch(room - QUAD, *block)] for _ in range(rings - 1)],
                scratch(rings, QUAD - 1, slots, *block),
                scratch(rings, slots, *block),
                pltpu.VMEM((2, hops, 6, time_count, 6 * sites), F32),
                pltpu.VMEM((hops, sites, 6 * sites), F32),
                scratch(share, *tile),
                scratch(share, *tile),
                scratch(share, *tile),
                scratch(share, *tile),
                scratch(rings, most, *tile),
                scratch(most, *tile),
                scratch(QUAD, most, *tile),
                pltpu.SemaphoreType.DMA((5,)),
            ]
            + both(2)
            + both(rings - 1, 2)
            + both(rings, QUAD - 1, slots)
            + [pltpu.SemaphoreType.DMA((rings, slots))]
            + both(1)
            + both(share)
            + [pltpu.SemaphoreType.DMA((share,)), pltpu.SemaphoreType.DMA((rings, most))]
            + both(QUAD - 1, most),
            compiler_params=pltpu.CompilerParams(
                collective_id=room, has_side_effects=True, vmem_limit_bytes=56 * 2**20
            ),
            name=f"exchange{room}",
        )

    least, most = QUAD + 1, QUAD * slots
    filled = (owned_times.reshape(rings, -1) >= 0).astype(jnp.int32)
    worst = jnp.max(jnp.sum(filled, 1))
    blocks, elem = lax.switch(
        jnp.clip(worst - least, 0, most - least),
        [exchange(room) for room in range(least, most + 1)],
        owned_times.T, hop_path, *arrays,
    )
    return pl.pallas_call(
        triple_kernel,
        grid=(slots, groups),
        out_shape=jax.ShapeDtypeStruct((slots, groups, 2, order, order), BF16),
        in_specs=[
            smem,
            smem,
            smem,
            pl.BlockSpec((1, n, 2, rows, order), lambda s, g: (s, 0, 0, 0, 0)),
            pl.BlockSpec((1, width, 2 * width), lambda s, g: (s, 0, 0)),
        ],
        out_specs=pl.BlockSpec((1, 1, 2, order, order), lambda s, g: (s, g, 0, 0, 0)),
        scratch_shapes=[
            pltpu.VMEM((order, 2 * order), BF16),
            pltpu.VMEM((order // width, 2, width, order), BF16),
        ],
        compiler_params=pltpu.CompilerParams(
            dimension_semantics=("arbitrary", "arbitrary"), vmem_limit_bytes=56 * 2**20
        ),
        name="triple",
    )(spin_perm, spin_phase, owned_times.T, blocks, elem)


def solution(mesh):
    in_specs = (
        P("groups", None, None, "src", None, None, None),
        P("groups", None, None, None, None, "src", None, None),
        P("groups"),
        P("groups", None),
        P("groups", None),
        P("groups", None, "src", None),
        P("groups", None),
    )
    out_specs = P(("groups", "src"), None, None, None, None)
    return jax.shard_map(
        functools.partial(shards, mesh.shape["src"]),
        mesh=mesh, in_specs=in_specs, out_specs=out_specs, check_vma=False,
    )
```

```python
import functools

import jax
import jax.numpy as jnp
import numpy as np
from jax import lax
from jax.experimental import pallas as pl
from jax.experimental.pallas import tpu as pltpu
from jax.sharding import PartitionSpec as P

F32 = jnp.float32
BF16 = jnp.bfloat16
QUAD = 4


def site_tables(side_y, side_z):
    sites = side_y * side_z
    site = np.arange(sites)
    ypos, zpos = site // side_z, site % side_z
    up_y = ((ypos + 1) % side_y) * side_z + zpos
    up_z = ypos * side_z + (zpos + 1) % side_z
    masks, movers = [], []
    for target in (up_y, up_z):
        up = (target[:, None] == site[None, :]).astype(np.float32)
        masks += [up, up.T]
        movers += [up, np.eye(sites, dtype=np.float32)]
    masks = np.stack([np.tile(m, (1, 6)) for m in masks])
    movers = np.stack([np.kron(np.eye(6, dtype=np.float32), m) for m in movers])
    return masks, movers


def flip(index, mask):
    result, bit = index, 1
    while bit <= mask:
        if mask & bit:
            result = result + bit - 2 * bit * lax.rem(index // bit, 2)
        bit *= 2
    return result


def schedule(rings):
    far = rings // 2
    rest = [m for m in reversed(range(2, rings)) if m != far]

    def each(step, masks):
        return [(step, m, part) for m in masks for part in range(2)]

    return (
        (each("send", [1] + rest + [far]), each("send", [1] + rest)),
        each("pass", [0]) + [("theirs",), ("ours",), ("join",)],
        (each("pass", [1]), each("pass", [1] + rest)),
        [("cross",)],
        (each("pass", rest), each("send", [far]) + each("pass", [far])),
        [("spread",)],
        (each("pass", [far]), []),
        [("collect",)],
    )


def exchange_kernel(
    n, hops, room, owned_ref, hop_ref, pera_hbm, eig_hbm, links_hbm, masks_hbm, movers_hbm,
    blocks_ref, elem_ref,
    pera_ref, eig_ref, links_ref, masks_ref, movers_ref, table, place, zstage, zland, fstage, mine, rows_ref, hopmask,
    esend, work, ypart, joined, across, whole, picked,
    fetch, give, take, zsend, zrecv, fsend, frecv, flocal, ysend, yrecv, jsend, jrecv, csend, crecv, psend, precv,
):
    slots = blocks_ref.shape[0]
    time_count = pera_ref.shape[0]
    rings = n // QUAD
    share = rings * room // QUAD
    most = -(-room // QUAD)
    me, group = lax.axis_index("src"), lax.axis_index("groups")
    mine_q, mine_z = lax.rem(me, QUAD), me // QUAD

    def at_quad(mask):
        return (group, mine_z * QUAD + flip(mine_q, mask))

    def at_ring(mask):
        return (group, flip(mine_z, mask) * QUAD + mine_q)

    def remote(src, dst, send, recv, device):
        return pltpu.make_async_remote_copy(src_ref=src, dst_ref=dst, send_sem=send, recv_sem=recv, device_id=device)

    pairs = (
        (pera_hbm, pera_ref), (links_hbm, links_ref.at[0]), (masks_hbm, masks_ref), (movers_hbm, movers_ref),
        (eig_hbm, eig_ref.at[0]),
    )
    fetches = [pltpu.make_async_copy(src, dst, fetch.at[i]) for i, (src, dst) in enumerate(pairs)]
    for copy in fetches:
        copy.start()

    barrier = pltpu.get_barrier_semaphore()
    for mask in range(1, QUAD):
        pl.semaphore_signal(barrier, inc=1, device_id=at_quad(mask))
    for mask in range(1, rings):
        pl.semaphore_signal(barrier, inc=1, device_id=at_ring(mask))

    @pl.loop(0, rings)
    def _(z):
        count = jnp.int32(0)
        found = [jnp.int32(0)] * room
        for s in range(slots):
            for q in range(QUAD):
                time = owned_ref[s, z * QUAD + q]
                filled = time >= 0
                place[s, z * QUAD + q] = jnp.minimum(count, room - 1)
                for j in range(min(room, s * QUAD + q + 1)):
                    found[j] = jnp.where(jnp.logical_and(filled, count == j), time, found[j])
                count = count + filled.astype(jnp.int32)
        for j in range(room):
            table[z * room + j] = found[j]

    fetches[0].wait()

    def stage_ring(mask):
        z = flip(mine_z, mask)
        for j in range(room):
            zstage[mask - 1, j] = pera_ref[table[z * room + j]]

    spans = ((0, QUAD), (QUAD, room - QUAD))

    def ring_copy(mask, part):
        first, size = spans[part]
        return remote(
            zstage.at[mask - 1, pl.ds(first, size)], zland[mask - 1][part],
            zsend.at[mask - 1, part], zrecv.at[mask - 1, part], at_ring(mask),
        )

    def quad_copy(ring, mask, s, receive):
        column = flip(mine_z, ring) * QUAD + (flip(mine_q, mask) if receive else mine_q)
        target = flip(mine_z, ring) * QUAD + mine_q
        return remote(
            fstage.at[ring, mask - 1, s], blocks_ref.at[s, column if receive else target],
            fsend.at[ring, mask - 1, s], frecv.at[ring, mask - 1, s], at_quad(mask),
        )

    def own_copy(ring, s):
        target = flip(mine_z, ring) * QUAD + mine_q
        return pltpu.make_async_copy(mine.at[ring, s], blocks_ref.at[s, target], flocal.at[ring, s])

    def forward(ring, s):
        def entry(q):
            at = place[s, mine_z * QUAD + q]
            if ring == 0:
                return pera_ref[table[mine_z * room + at]]
            first, rest = zland[ring - 1]
            value = first[jnp.minimum(at, QUAD - 1)]
            if s > 0:
                value = jnp.where(at < QUAD, value, rest[jnp.maximum(at - QUAD, 0)])
            return value

        for mask in range(1, QUAD):
            fstage[ring, mask - 1, s] = entry(flip(mine_q, mask))
            quad_copy(ring, mask, s, False).start()
        mine[ring, s] = entry(mine_q)
        own_copy(ring, s).start()

    pl.semaphore_wait(barrier, QUAD + rings - 2)
    shares = [
        remote(eig_hbm, eig_ref.at[1], give.at[0], take.at[0], at_quad(1)),
        remote(links_hbm, links_ref.at[1], give.at[1], take.at[1], at_quad(1)),
    ]
    for copy in shares:
        copy.start()
    def send_ring(mask, part):
        if part == 0:
            stage_ring(mask)
        ring_copy(mask, part).start()

    def pass_on(mask, s):
        if mask:
            ring_copy(mask, s).wait_recv()
        forward(mask, s)

    def one_plane(plane, time):
        vec = eig_ref[plane, time]
        cur = vec
        mid = vec.shape[0] // 2
        for h in range(hops):
            mask = hopmask[h]
            hop = [mask * rows_ref[plane, h, j, pl.ds(time, 1), :] for j in range(6)]
            cur = jnp.dot(jnp.concatenate(hop, 0).astype(BF16), cur, preferred_element_type=F32).astype(BF16)
        turned = jnp.concatenate([cur[mid:], -cur[:mid]], 0)
        return vec, jnp.concatenate([cur, turned], 1)

    def one_entry(entry):
        time = table[entry]
        left, right = zip(*(one_plane(plane, time) for plane in range(2)))
        return lax.dot_general(
            jnp.concatenate(left, 0), jnp.concatenate(right, 0), (((0,), (0,)), ((), ())), preferred_element_type=F32
        ).astype(BF16)

    def theirs(i, carry):
        esend[i] = one_entry(QUAD * i + flip(mine_q, 2))
        return carry

    def ours(i, carry):
        work[i] = one_entry(QUAD * i + mine_q)
        return carry

    y_copy = remote(esend, ypart, ysend.at[0], yrecv.at[0], at_quad(2))

    def row_of(i):
        return (QUAD * i + mine_q) // room

    def first_of(z):
        return (z * room - mine_q + QUAD - 1) // QUAD

    def even(i):
        return lax.rem(row_of(i) + mine_z, 2) == 0

    def join_copy(i):
        return remote(work.at[i], joined.at[i], jsend.at[i], jrecv.at[i], at_ring(1))

    def cross_copy(i):
        z = row_of(i)
        at = i - first_of(z)
        return remote(work.at[i], across.at[mine_z, at], csend.at[i], crecv.at[mine_z, at], (group, z * QUAD + mine_q))

    def cross_land(z, at):
        return remote(work.at[0], across.at[z, at], csend.at[0], crecv.at[z, at], (group, z * QUAD + mine_q))

    def held(at):
        return first_of(mine_z) + at < first_of(mine_z + 1)

    def pick_copy(mask, origin, at):
        return remote(
            whole.at[at], picked.at[origin, at], psend.at[mask - 1, at], precv.at[mask - 1, at], at_quad(mask)
        )

    def compute_theirs():
        for copy in fetches[1:]:
            copy.wait()
        for copy in shares:
            copy.wait()
        for h in range(hops):
            code = hop_ref[h]
            chosen = [(code == i).astype(F32) for i in range(4)]
            hopmask[h] = sum(chosen[i] * masks_ref[i] for i in range(4))
            mover = sum(chosen[i] * movers_ref[i] for i in range(4)).astype(BF16)
            for plane in range(2):
                for k in range(2):
                    for c in range(3):
                        stack = []
                        for part in range(2):
                            kind = (k + part) % 2
                            turn = -1.0 if part == 1 and kind == 1 else 1.0
                            sign = turn * (1.0 - 2.0 * kind)
                            for d in range(3):
                                here, there = kind * 9 + c * 3 + d, kind * 9 + d * 3 + c
                                stack.append(
                                    (turn * chosen[0]) * links_ref[plane, here].astype(F32)
                                    + (sign * chosen[1]) * links_ref[plane, there].astype(F32)
                                    + (turn * chosen[2]) * links_ref[plane, 18 + here].astype(F32)
                                    + (sign * chosen[3]) * links_ref[plane, 18 + there].astype(F32)
                                )
                        rows_ref[plane, h, k * 3 + c] = lax.dot_general(
                            jnp.concatenate(stack, 0).astype(BF16), mover, (((0,), (0,)), ((), ())),
                            preferred_element_type=F32,
                        )

        lax.fori_loop(0, share, theirs, 0, unroll=2)
        y_copy.start()

    def compute_ours():
        lax.fori_loop(0, share, ours, 0, unroll=2)

    def join():
        y_copy.wait()

        @pl.loop(0, share)
        def _(i):
            @pl.when(jnp.logical_not(even(i)))
            def _():
                work[i] = (work[i].astype(F32) + ypart[i].astype(F32)).astype(BF16)
                join_copy(i).start()

    def cross():
        @pl.loop(0, share)
        def _(i):
            @pl.when(even(i))
            def _():
                join_copy(i).wait_recv()
                total = work[i].astype(F32) + ypart[i].astype(F32) + joined[i].astype(F32)
                work[i] = total.astype(BF16)

                @pl.when(row_of(i) != mine_z)
                def _():
                    cross_copy(i).start()

    def spread():
        for at in range(most):

            @pl.when(held(at))
            def _():
                total = work[first_of(mine_z) + at].astype(F32)
                for mask in range(2, rings, 2):
                    z = flip(mine_z, mask)
                    cross_land(z, at).wait_recv()
                    total += across[z, at].astype(F32)
                whole[at] = total.astype(BF16)
                for mask in range(1, QUAD):
                    pick_copy(mask, mine_q, at).start()
                picked[mine_q, at] = whole[at]

    def collect():
        @pl.loop(0, share)
        def _(i):
            @pl.when(jnp.logical_not(even(i)))
            def _():
                join_copy(i).wait_send()

            @pl.when(jnp.logical_and(even(i), row_of(i) != mine_z))
            def _():
                cross_copy(i).wait_send()

        for mask in range(1, QUAD):
            q = flip(mine_q, mask)
            for at in range(most):

                @pl.when(held(at))
                def _():
                    pick_copy(mask, mine_q, at).wait_send()

                @pl.when((mine_z * room - q + QUAD - 1) // QUAD + at < ((mine_z + 1) * room - q + QUAD - 1) // QUAD)
                def _():
                    pick_copy(mask, q, at).wait_recv()

        for s in range(slots):
            entry = mine_z * room + place[s, me]
            q = lax.rem(entry, QUAD)
            first = lax.div(mine_z * room - q + QUAD - 1, QUAD)
            elem_ref[s] = picked[q, jnp.maximum(lax.div(entry, QUAD) - first, 0)]

    actions = {
        "send": send_ring, "pass": pass_on, "theirs": compute_theirs, "ours": compute_ours, "join": join,
        "cross": cross, "spread": spread, "collect": collect,
    }

    def run(steps):
        for name, *rest in steps:
            actions[name](*rest)

    inner = jnp.logical_and(mine_z > 0, mine_z < rings - 1)
    for phase in schedule(rings):
        if isinstance(phase, tuple):
            pl.when(jnp.logical_not(inner))(functools.partial(run, phase[0]))
            pl.when(inner)(functools.partial(run, phase[1]))
        else:
            run(phase)

    for mask in range(1, rings):
        for part in range(2):
            ring_copy(mask, part).wait_send()
    for ring in range(rings):
        for s in range(slots):
            for mask in range(1, QUAD):
                quad_copy(ring, mask, s, False).wait_send()
                quad_copy(ring, mask, s, True).wait_recv()
            own_copy(ring, s).wait()


def triple_kernel(perm_ref, phase_ref, owned_ref, blocks_ref, elem_ref, out_ref, left, turned):
    slot = pl.program_id(0)
    order = out_ref.shape[-1]
    width = elem_ref.shape[1]
    spins = order // width
    elem = elem_ref[0]
    re = blocks_ref[0, :, 0].reshape(order, order)
    im = blocks_ref[0, :, 1].reshape(order, order)
    left[:, :order] = re
    left[:, order:] = im
    for spin in range(spins):
        part_re = re[:, spin * width : (spin + 1) * width]
        part_im = im[:, spin * width : (spin + 1) * width]
        dims = (((1,), (1,)), ((), ()))
        turned[spin, 0] = lax.dot_general(
            elem, jnp.concatenate([part_re, -part_im], 1), dims, preferred_element_type=F32
        ).astype(BF16)
        turned[spin, 1] = lax.dot_general(
            elem, jnp.concatenate([part_im, part_re], 1), dims, preferred_element_type=F32
        ).astype(BF16)
    filled = (owned_ref[slot, lax.axis_index("src")] >= 0).astype(F32)

    def spread(scale):
        return jnp.full((width, order), scale * filled, F32).astype(BF16)

    for group in range(perm_ref.shape[0]):
        reals, imags = [], []
        for spin in range(spins):
            source = perm_ref[group, spin]
            phase = phase_ref[group, spin]
            scale_re = spread((phase == 0).astype(F32) - (phase == 2).astype(F32))
            scale_im = spread((phase == 1).astype(F32) - (phase == 3).astype(F32))
            part_re = turned[source, 0]
            part_im = turned[source, 1]
            reals.append(scale_re * part_re - scale_im * part_im)
            imags.append(scale_re * part_im + scale_im * part_re)
        real, imag = jnp.concatenate(reals, 0), jnp.concatenate(imags, 0)
        for part, right in enumerate((jnp.concatenate([real, imag], 0), jnp.concatenate([imag, -real], 0))):
            for half in range(2):
                columns = slice(half * order // 2, (half + 1) * order // 2)
                out_ref[0, group, part, :, columns] = jnp.dot(
                    left[...], right[:, columns], preferred_element_type=F32
                ).astype(BF16)


def shards(n, eigenvectors, gauge_links, hop_path, spin_perm, spin_phase, perambulators, owned_times):
    time_count = eigenvectors.shape[0]
    width = eigenvectors.shape[-1]
    slots = owned_times.shape[1]
    rows, order = perambulators.shape[2], perambulators.shape[3]
    groups = spin_perm.shape[0]
    hops = hop_path.shape[0]
    rings = n // QUAD
    side_y, side_z = eigenvectors.shape[4], eigenvectors.shape[5]
    sites = side_y * side_z
    eig = eigenvectors.reshape(time_count, -1, width)
    links = jnp.transpose(gauge_links.reshape(time_count, 36, sites), (1, 2, 0))
    masks, movers = site_tables(side_y, side_z)
    tile = (width, 2 * width)
    block = (2, rows, order)
    vmem = pl.BlockSpec(memory_space=pltpu.VMEM)
    smem = pl.BlockSpec(memory_space=pltpu.SMEM)
    arrays = (perambulators, eig, links, jnp.asarray(masks), jnp.asarray(movers))

    def exchange(room):
        share = rings * room // QUAD
        most = -(-room // QUAD)

        def scratch(*shape):
            return pltpu.VMEM(shape, BF16)

        def both(*shape):
            return [pltpu.SemaphoreType.DMA(shape)] * 2

        return pl.pallas_call(
            functools.partial(exchange_kernel, n, hops, room),
            out_shape=(
                jax.ShapeDtypeStruct((slots, n) + block, BF16),
                jax.ShapeDtypeStruct((slots,) + tile, BF16),
            ),
            in_specs=[smem, smem] + [pl.BlockSpec(memory_space=pltpu.HBM)] * 5,
            out_specs=(pl.BlockSpec(memory_space=pl.ANY), vmem),
            scratch_shapes=[
                scratch(*perambulators.shape),
                scratch(2, *eig.shape),
                scratch(2, *links.shape),
                pltpu.VMEM(masks.shape, F32),
                pltpu.VMEM(movers.shape, F32),
                pltpu.SMEM((rings * room,), jnp.int32),
                pltpu.SMEM((slots, n), jnp.int32),
                scratch(rings - 1, room, *block),
                [[scratch(QUAD, *block), scratch(room - QUAD, *block)] for _ in range(rings - 1)],
                scratch(rings, QUAD - 1, slots, *block),
                scratch(rings, slots, *block),
                pltpu.VMEM((2, hops, 6, time_count, 6 * sites), F32),
                pltpu.VMEM((hops, sites, 6 * sites), F32),
                scratch(share, *tile),
                scratch(share, *tile),
                scratch(share, *tile),
                scratch(share, *tile),
                scratch(rings, most, *tile),
                scratch(most, *tile),
                scratch(QUAD, most, *tile),
                pltpu.SemaphoreType.DMA((5,)),
            ]
            + both(2)
            + both(rings - 1, 2)
            + both(rings, QUAD - 1, slots)
            + [pltpu.SemaphoreType.DMA((rings, slots))]
            + both(1)
            + both(share)
            + [pltpu.SemaphoreType.DMA((share,)), pltpu.SemaphoreType.DMA((rings, most))]
            + both(QUAD - 1, most),
            compiler_params=pltpu.CompilerParams(
                collective_id=room, has_side_effects=True, vmem_limit_bytes=56 * 2**20
            ),
            name=f"exchange{room}",
        )

    least, most = QUAD + 1, QUAD * slots
    filled = (owned_times.reshape(rings, -1) >= 0).astype(jnp.int32)
    worst = jnp.max(sum(filled[:, j] for j in range(most)))
    blocks, elem = lax.switch(
        jnp.clip(worst - least, 0, most - least),
        [exchange(room) for room in range(least, most + 1)],
        owned_times.T, hop_path, *arrays,
    )
    return pl.pallas_call(
        triple_kernel,
        grid=(slots,),
        out_shape=jax.ShapeDtypeStruct((slots, groups, 2, order, order), BF16),
        in_specs=[
            smem,
            smem,
            smem,
            pl.BlockSpec((1, n, 2, rows, order), lambda s: (s, 0, 0, 0, 0)),
            pl.BlockSpec((1, width, 2 * width), lambda s: (s, 0, 0)),
        ],
        out_specs=pl.BlockSpec((1, groups, 2, order, order), lambda s: (s, 0, 0, 0, 0)),
        scratch_shapes=[
            pltpu.VMEM((order, 2 * order), BF16),
            pltpu.VMEM((order // width, 2, width, order), BF16),
        ],
        compiler_params=pltpu.CompilerParams(
            dimension_semantics=("arbitrary",), vmem_limit_bytes=56 * 2**20
        ),
        name="triple",
    )(spin_perm, spin_phase, owned_times.T, blocks, elem)


def solution(mesh):
    in_specs = (
        P("groups", None, None, "src", None, None, None),
        P("groups", None, None, None, None, "src", None, None),
        P("groups"),
        P("groups", None),
        P("groups", None),
        P("groups", None, "src", None),
        P("groups", None),
    )
    out_specs = P(("groups", "src"), None, None, None, None)
    return jax.shard_map(
        functools.partial(shards, mesh.shape["src"]),
        mesh=mesh, in_specs=in_specs, out_specs=out_specs, check_vma=False,
    )
```

```python
import functools

import jax
import jax.numpy as jnp
import numpy as np
from jax import lax
from jax.experimental import pallas as pl
from jax.experimental.pallas import tpu as pltpu
from jax.sharding import PartitionSpec as P

F32 = jnp.float32
BF16 = jnp.bfloat16
QUAD = 4


def site_tables(side_y, side_z):
    sites = side_y * side_z
    site = np.arange(sites)
    ypos, zpos = site // side_z, site % side_z
    up_y = ((ypos + 1) % side_y) * side_z + zpos
    up_z = ypos * side_z + (zpos + 1) % side_z
    masks, movers = [], []
    for target in (up_y, up_z):
        up = (target[:, None] == site[None, :]).astype(np.float32)
        masks += [up, up.T]
        movers += [up, np.eye(sites, dtype=np.float32)]
    masks = np.stack([np.tile(m, (1, 6)) for m in masks])
    movers = np.stack([np.kron(np.eye(6, dtype=np.float32), m) for m in movers])
    return masks, movers


def flip(index, mask):
    result, bit = index, 1
    while bit <= mask:
        if mask & bit:
            result = result + bit - 2 * bit * lax.rem(index // bit, 2)
        bit *= 2
    return result


def schedule(rings):
    far = rings // 2
    rest = [m for m in reversed(range(2, rings)) if m != far]

    def each(step, masks):
        return [(step, m, part) for m in masks for part in range(2)]

    return (
        (each("send", [1] + rest + [far]), each("send", [1] + rest)),
        each("pass", [0]) + [("theirs",), ("ours",), ("join",)],
        (each("pass", [1]), each("pass", [1] + rest)),
        [("cross",)],
        (each("pass", rest), each("send", [far]) + each("pass", [far])),
        [("spread",)],
        (each("pass", [far]), []),
        [("collect",)],
    )


def exchange_kernel(
    n, hops, room, owned_ref, hop_ref, pera_hbm, eig_hbm, links_hbm, masks_hbm, movers_hbm,
    blocks_ref, elem_ref,
    pera_ref, eig_ref, links_ref, masks_ref, movers_ref, table, place, zstage, zland, fstage, mine, rows_ref, hopmask,
    esend, work, ypart, joined, across, whole, picked,
    fetch, give, take, zsend, zrecv, fsend, frecv, flocal, ysend, yrecv, jsend, jrecv, csend, crecv, psend, precv,
):
    slots = blocks_ref.shape[0]
    time_count = pera_ref.shape[0]
    rings = n // QUAD
    share = rings * room // QUAD
    most = -(-room // QUAD)
    me, group = lax.axis_index("src"), lax.axis_index("groups")
    mine_q, mine_z = lax.rem(me, QUAD), me // QUAD

    def at_quad(mask):
        return (group, mine_z * QUAD + flip(mine_q, mask))

    def at_ring(mask):
        return (group, flip(mine_z, mask) * QUAD + mine_q)

    def remote(src, dst, send, recv, device):
        return pltpu.make_async_remote_copy(src_ref=src, dst_ref=dst, send_sem=send, recv_sem=recv, device_id=device)

    pairs = (
        (pera_hbm, pera_ref), (links_hbm, links_ref.at[0]), (masks_hbm, masks_ref), (movers_hbm, movers_ref),
        (eig_hbm, eig_ref.at[0]),
    )
    fetches = [pltpu.make_async_copy(src, dst, fetch.at[i]) for i, (src, dst) in enumerate(pairs)]
    for copy in fetches:
        copy.start()

    barrier = pltpu.get_barrier_semaphore()
    for mask in range(1, QUAD):
        pl.semaphore_signal(barrier, inc=1, device_id=at_quad(mask))
    for mask in range(1, rings):
        pl.semaphore_signal(barrier, inc=1, device_id=at_ring(mask))

    @pl.loop(0, rings)
    def _(z):
        count = jnp.int32(0)
        found = [jnp.int32(0)] * room
        for s in range(slots):
            for q in range(QUAD):
                time = owned_ref[s, z * QUAD + q]
                filled = time >= 0
                place[s, z * QUAD + q] = jnp.minimum(count, room - 1)
                for j in range(min(room, s * QUAD + q + 1)):
                    found[j] = jnp.where(jnp.logical_and(filled, count == j), time, found[j])
                count = count + filled.astype(jnp.int32)
        for j in range(room):
            table[z * room + j] = found[j]

    fetches[0].wait()

    def stage_ring(mask):
        z = flip(mine_z, mask)
        for j in range(room):
            zstage[mask - 1, j] = pera_ref[table[z * room + j]]

    spans = ((0, QUAD), (QUAD, room - QUAD))

    def ring_copy(mask, part):
        first, size = spans[part]
        return remote(
            zstage.at[mask - 1, pl.ds(first, size)], zland[mask - 1][part],
            zsend.at[mask - 1, part], zrecv.at[mask - 1, part], at_ring(mask),
        )

    def quad_copy(ring, mask, s, receive):
        column = flip(mine_z, ring) * QUAD + (flip(mine_q, mask) if receive else mine_q)
        target = flip(mine_z, ring) * QUAD + mine_q
        return remote(
            fstage.at[ring, mask - 1, s], blocks_ref.at[s, column if receive else target],
            fsend.at[ring, mask - 1, s], frecv.at[ring, mask - 1, s], at_quad(mask),
        )

    def own_copy(ring, s):
        target = flip(mine_z, ring) * QUAD + mine_q
        return pltpu.make_async_copy(mine.at[ring, s], blocks_ref.at[s, target], flocal.at[ring, s])

    def forward(ring, s):
        def entry(q):
            at = place[s, mine_z * QUAD + q]
            if ring == 0:
                return pera_ref[table[mine_z * room + at]]
            first, rest = zland[ring - 1]
            value = first[jnp.minimum(at, QUAD - 1)]
            if s > 0:
                value = jnp.where(at < QUAD, value, rest[jnp.maximum(at - QUAD, 0)])
            return value

        for mask in range(1, QUAD):
            fstage[ring, mask - 1, s] = entry(flip(mine_q, mask))
            quad_copy(ring, mask, s, False).start()
        mine[ring, s] = entry(mine_q)
        own_copy(ring, s).start()

    pl.semaphore_wait(barrier, QUAD + rings - 2)
    shares = [
        remote(eig_hbm, eig_ref.at[1], give.at[0], take.at[0], at_quad(1)),
        remote(links_hbm, links_ref.at[1], give.at[1], take.at[1], at_quad(1)),
    ]
    for copy in shares:
        copy.start()
    def send_ring(mask, part):
        if part == 0:
            stage_ring(mask)
        ring_copy(mask, part).start()

    def pass_on(mask, s):
        if mask:
            ring_copy(mask, s).wait_recv()
        forward(mask, s)

    def one_plane(plane, time):
        vec = eig_ref[plane, time]
        cur = vec
        mid = vec.shape[0] // 2
        for h in range(hops):
            mask = hopmask[h]
            hop = [mask * rows_ref[plane, h, j, pl.ds(time, 1), :] for j in range(6)]
            cur = jnp.dot(jnp.concatenate(hop, 0).astype(BF16), cur, preferred_element_type=F32).astype(BF16)
        turned = jnp.concatenate([cur[mid:], -cur[:mid]], 0)
        return vec, jnp.concatenate([cur, turned], 1)

    def one_entry(entry):
        time = table[entry]
        left, right = zip(*(one_plane(plane, time) for plane in range(2)))
        return lax.dot_general(
            jnp.concatenate(left, 0), jnp.concatenate(right, 0), (((0,), (0,)), ((), ())), preferred_element_type=F32
        ).astype(BF16)

    def theirs(i, carry):
        esend[i] = one_entry(QUAD * i + flip(mine_q, 2))
        return carry

    def ours(i, carry):
        work[i] = one_entry(QUAD * i + mine_q)
        return carry

    y_copy = remote(esend, ypart, ysend.at[0], yrecv.at[0], at_quad(2))

    def row_of(i):
        return (QUAD * i + mine_q) // room

    def first_of(z):
        return (z * room - mine_q + QUAD - 1) // QUAD

    def even(i):
        return lax.rem(row_of(i) + mine_z, 2) == 0

    def join_copy(i):
        return remote(work.at[i], joined.at[i], jsend.at[i], jrecv.at[i], at_ring(1))

    def cross_copy(i):
        z = row_of(i)
        at = i - first_of(z)
        return remote(work.at[i], across.at[mine_z, at], csend.at[i], crecv.at[mine_z, at], (group, z * QUAD + mine_q))

    def cross_land(z, at):
        return remote(work.at[0], across.at[z, at], csend.at[0], crecv.at[z, at], (group, z * QUAD + mine_q))

    def held(at):
        return first_of(mine_z) + at < first_of(mine_z + 1)

    def pick_copy(mask, origin, at):
        return remote(
            whole.at[at], picked.at[origin, at], psend.at[mask - 1, at], precv.at[mask - 1, at], at_quad(mask)
        )

    def compute_theirs():
        for copy in fetches[1:]:
            copy.wait()
        for copy in shares:
            copy.wait()
        for h in range(hops):
            code = hop_ref[h]
            chosen = [(code == i).astype(F32) for i in range(4)]
            hopmask[h] = sum(chosen[i] * masks_ref[i] for i in range(4))
            mover = sum(chosen[i] * movers_ref[i] for i in range(4)).astype(BF16)
            for plane in range(2):
                for k in range(2):
                    for c in range(3):
                        stack = []
                        for part in range(2):
                            kind = (k + part) % 2
                            turn = -1.0 if part == 1 and kind == 1 else 1.0
                            sign = turn * (1.0 - 2.0 * kind)
                            for d in range(3):
                                here, there = kind * 9 + c * 3 + d, kind * 9 + d * 3 + c
                                stack.append(
                                    (turn * chosen[0]) * links_ref[plane, here].astype(F32)
                                    + (sign * chosen[1]) * links_ref[plane, there].astype(F32)
                                    + (turn * chosen[2]) * links_ref[plane, 18 + here].astype(F32)
                                    + (sign * chosen[3]) * links_ref[plane, 18 + there].astype(F32)
                                )
                        rows_ref[plane, h, k * 3 + c] = lax.dot_general(
                            jnp.concatenate(stack, 0).astype(BF16), mover, (((0,), (0,)), ((), ())),
                            preferred_element_type=F32,
                        )

        lax.fori_loop(0, share, theirs, 0, unroll=2)
        y_copy.start()

    def compute_ours():
        lax.fori_loop(0, share, ours, 0, unroll=2)

    def join():
        y_copy.wait()

        @pl.loop(0, share)
        def _(i):
            @pl.when(jnp.logical_not(even(i)))
            def _():
                work[i] = (work[i].astype(F32) + ypart[i].astype(F32)).astype(BF16)
                join_copy(i).start()

    def cross():
        @pl.loop(0, share)
        def _(i):
            @pl.when(even(i))
            def _():
                join_copy(i).wait_recv()
                total = work[i].astype(F32) + ypart[i].astype(F32) + joined[i].astype(F32)
                work[i] = total.astype(BF16)

                @pl.when(row_of(i) != mine_z)
                def _():
                    cross_copy(i).start()

    def spread():
        for at in range(most):

            @pl.when(held(at))
            def _():
                total = work[first_of(mine_z) + at].astype(F32)
                for mask in range(2, rings, 2):
                    z = flip(mine_z, mask)
                    cross_land(z, at).wait_recv()
                    total += across[z, at].astype(F32)
                whole[at] = total.astype(BF16)
                for mask in range(1, QUAD):
                    pick_copy(mask, mine_q, at).start()
                picked[mine_q, at] = whole[at]

    def collect():
        @pl.loop(0, share)
        def _(i):
            @pl.when(jnp.logical_not(even(i)))
            def _():
                join_copy(i).wait_send()

            @pl.when(jnp.logical_and(even(i), row_of(i) != mine_z))
            def _():
                cross_copy(i).wait_send()

        for mask in range(1, QUAD):
            q = flip(mine_q, mask)
            for at in range(most):

                @pl.when(held(at))
                def _():
                    pick_copy(mask, mine_q, at).wait_send()

                @pl.when((mine_z * room - q + QUAD - 1) // QUAD + at < ((mine_z + 1) * room - q + QUAD - 1) // QUAD)
                def _():
                    pick_copy(mask, q, at).wait_recv()

        for s in range(slots):
            entry = mine_z * room + place[s, me]
            q = lax.rem(entry, QUAD)
            first = lax.div(mine_z * room - q + QUAD - 1, QUAD)
            elem_ref[s] = picked[q, jnp.maximum(lax.div(entry, QUAD) - first, 0)]

    actions = {
        "send": send_ring, "pass": pass_on, "theirs": compute_theirs, "ours": compute_ours, "join": join,
        "cross": cross, "spread": spread, "collect": collect,
    }

    def run(steps):
        for name, *rest in steps:
            actions[name](*rest)

    inner = jnp.logical_and(mine_z > 0, mine_z < rings - 1)
    for phase in schedule(rings):
        if isinstance(phase, tuple):
            pl.when(jnp.logical_not(inner))(functools.partial(run, phase[0]))
            pl.when(inner)(functools.partial(run, phase[1]))
        else:
            run(phase)

    for mask in range(1, rings):
        for part in range(2):
            ring_copy(mask, part).wait_send()
    for ring in range(rings):
        for s in range(slots):
            for mask in range(1, QUAD):
                quad_copy(ring, mask, s, False).wait_send()
                quad_copy(ring, mask, s, True).wait_recv()
            own_copy(ring, s).wait()


def triple_kernel(perm_ref, phase_ref, owned_ref, blocks_ref, elem_ref, out_ref, left, turned):
    slot = pl.program_id(0)
    order = out_ref.shape[-1]
    width = elem_ref.shape[1]
    spins = order // width
    elem = elem_ref[0]
    re = blocks_ref[0, :, 0].reshape(order, order)
    im = blocks_ref[0, :, 1].reshape(order, order)
    left[:, :order] = re
    left[:, order:] = im
    for spin in range(spins):
        part_re = re[:, spin * width : (spin + 1) * width]
        part_im = im[:, spin * width : (spin + 1) * width]
        dims = (((1,), (1,)), ((), ()))
        turned[spin, 0] = lax.dot_general(
            elem, jnp.concatenate([part_re, -part_im], 1), dims, preferred_element_type=F32
        ).astype(BF16)
        turned[spin, 1] = lax.dot_general(
            elem, jnp.concatenate([part_im, part_re], 1), dims, preferred_element_type=F32
        ).astype(BF16)
    filled = (owned_ref[slot, lax.axis_index("src")] >= 0).astype(F32)

    def spread(scale):
        return jnp.full((width, order), scale * filled, F32).astype(BF16)

    for group in range(perm_ref.shape[0]):
        reals, imags = [], []
        for spin in range(spins):
            source = perm_ref[group, spin]
            phase = phase_ref[group, spin]
            scale_re = spread((phase == 0).astype(F32) - (phase == 2).astype(F32))
            scale_im = spread((phase == 1).astype(F32) - (phase == 3).astype(F32))
            part_re = turned[source, 0]
            part_im = turned[source, 1]
            reals.append(scale_re * part_re - scale_im * part_im)
            imags.append(scale_re * part_im + scale_im * part_re)
        real, imag = jnp.concatenate(reals, 0), jnp.concatenate(imags, 0)
        for part, right in enumerate((jnp.concatenate([real, imag], 0), jnp.concatenate([imag, -real], 0))):
            for half in range(2):
                columns = slice(half * order // 2, (half + 1) * order // 2)
                out_ref[0, group, part, :, columns] = jnp.dot(
                    left[...], right[:, columns], preferred_element_type=F32
                ).astype(BF16)


def room_kernel(span, owned_ref, index_ref):
    slots, n = owned_ref.shape

    def row(z, worst):
        count = jnp.int32(0)
        for s in range(slots):
            for q in range(QUAD):
                count = count + (owned_ref[s, z * QUAD + q] >= 0).astype(jnp.int32)
        return jnp.maximum(worst, count)

    worst = lax.fori_loop(0, n // QUAD, row, jnp.int32(0))
    index_ref[0] = jnp.minimum(jnp.maximum(worst - QUAD - 1, 0), span)


def shards(n, eigenvectors, gauge_links, hop_path, spin_perm, spin_phase, perambulators, owned_times):
    time_count = eigenvectors.shape[0]
    width = eigenvectors.shape[-1]
    slots = owned_times.shape[1]
    rows, order = perambulators.shape[2], perambulators.shape[3]
    groups = spin_perm.shape[0]
    hops = hop_path.shape[0]
    rings = n // QUAD
    side_y, side_z = eigenvectors.shape[4], eigenvectors.shape[5]
    sites = side_y * side_z
    eig = eigenvectors.reshape(time_count, -1, width)
    links = jnp.transpose(gauge_links.reshape(time_count, 36, sites), (1, 2, 0))
    masks, movers = site_tables(side_y, side_z)
    tile = (width, 2 * width)
    block = (2, rows, order)
    vmem = pl.BlockSpec(memory_space=pltpu.VMEM)
    smem = pl.BlockSpec(memory_space=pltpu.SMEM)
    arrays = (perambulators, eig, links, jnp.asarray(masks), jnp.asarray(movers))

    def exchange(room):
        share = rings * room // QUAD
        most = -(-room // QUAD)

        def scratch(*shape):
            return pltpu.VMEM(shape, BF16)

        def both(*shape):
            return [pltpu.SemaphoreType.DMA(shape)] * 2

        return pl.pallas_call(
            functools.partial(exchange_kernel, n, hops, room),
            out_shape=(
                jax.ShapeDtypeStruct((slots, n) + block, BF16),
                jax.ShapeDtypeStruct((slots,) + tile, BF16),
            ),
            in_specs=[smem, smem] + [pl.BlockSpec(memory_space=pltpu.HBM)] * 5,
            out_specs=(pl.BlockSpec(memory_space=pl.ANY), vmem),
            scratch_shapes=[
                scratch(*perambulators.shape),
                scratch(2, *eig.shape),
                scratch(2, *links.shape),
                pltpu.VMEM(masks.shape, F32),
                pltpu.VMEM(movers.shape, F32),
                pltpu.SMEM((rings * room,), jnp.int32),
                pltpu.SMEM((slots, n), jnp.int32),
                scratch(rings - 1, room, *block),
                [[scratch(QUAD, *block), scratch(room - QUAD, *block)] for _ in range(rings - 1)],
                scratch(rings, QUAD - 1, slots, *block),
                scratch(rings, slots, *block),
                pltpu.VMEM((2, hops, 6, time_count, 6 * sites), F32),
                pltpu.VMEM((hops, sites, 6 * sites), F32),
                scratch(share, *tile),
                scratch(share, *tile),
                scratch(share, *tile),
                scratch(share, *tile),
                scratch(rings, most, *tile),
                scratch(most, *tile),
                scratch(QUAD, most, *tile),
                pltpu.SemaphoreType.DMA((5,)),
            ]
            + both(2)
            + both(rings - 1, 2)
            + both(rings, QUAD - 1, slots)
            + [pltpu.SemaphoreType.DMA((rings, slots))]
            + both(1)
            + both(share)
            + [pltpu.SemaphoreType.DMA((share,)), pltpu.SemaphoreType.DMA((rings, most))]
            + both(QUAD - 1, most),
            compiler_params=pltpu.CompilerParams(
                collective_id=room, has_side_effects=True, vmem_limit_bytes=56 * 2**20
            ),
            name=f"exchange{room}",
        )

    least, most = QUAD + 1, QUAD * slots
    index = pl.pallas_call(
        functools.partial(room_kernel, most - least),
        out_shape=jax.ShapeDtypeStruct((1,), jnp.int32),
        in_specs=[smem],
        out_specs=smem,
        name="room",
    )(owned_times.T)
    blocks, elem = lax.switch(
        index[0],
        [exchange(room) for room in range(least, most + 1)],
        owned_times.T, hop_path, *arrays,
    )
    return pl.pallas_call(
        triple_kernel,
        grid=(slots,),
        out_shape=jax.ShapeDtypeStruct((slots, groups, 2, order, order), BF16),
        in_specs=[
            smem,
            smem,
            smem,
            pl.BlockSpec((1, n, 2, rows, order), lambda s: (s, 0, 0, 0, 0)),
            pl.BlockSpec((1, width, 2 * width), lambda s: (s, 0, 0)),
        ],
        out_specs=pl.BlockSpec((1, groups, 2, order, order), lambda s: (s, 0, 0, 0, 0)),
        scratch_shapes=[
            pltpu.VMEM((order, 2 * order), BF16),
            pltpu.VMEM((order // width, 2, width, order), BF16),
        ],
        compiler_params=pltpu.CompilerParams(
            dimension_semantics=("arbitrary",), vmem_limit_bytes=56 * 2**20
        ),
        name="triple",
    )(spin_perm, spin_phase, owned_times.T, blocks, elem)


def solution(mesh):
    in_specs = (
        P("groups", None, None, "src", None, None, None),
        P("groups", None, None, None, None, "src", None, None),
        P("groups"),
        P("groups", None),
        P("groups", None),
        P("groups", None, "src", None),
        P("groups", None),
    )
    out_specs = P(("groups", "src"), None, None, None, None)
    return jax.shard_map(
        functools.partial(shards, mesh.shape["src"]),
        mesh=mesh, in_specs=in_specs, out_specs=out_specs, check_vma=False,
    )
```
